32 devices in a mesh: row: 16 (over z, x, core), col: 2 (over y).
Axes of the slice: x: 2, y: 2, z: 4, core: 2. Of those that a mesh axis runs over, the one named last changes fastest.
Arguments:
- vectors: bfloat16 [8, 4096], P(None, ('row', 'col')), may hold values from -16 to 16, as said below
- tile_vals: bfloat16 [16, 2, 3, 4, 128, 128], P('row', 'col'), may hold values from -0.375 to 0.375
- tile_rows: int32 [16, 2, 3, 4], P('row', 'col'), may hold values from 0 to 1, as said below
- tile_cols: int32 [16, 2, 3, 4], P('row', 'col'), may hold values from 0 to 15, as said below
- tile_counts: int32 [16, 2, 3], P('row', 'col'), may hold values from 1 to 4, as said below
- tile_diag: int32 [16, 2, 3, 4], P('row', 'col'), may hold values from 0 to 1, as said below
Outputs:
- applied: float32 [3, 8, 4096], P(None, None, ('row', 'col'))
- subspace: float32 [3, 8, 8], replicated
The draws below stay inside these ranges and needn't reach their ends.
Inputs may be any that keep to these rules, and one draw needn't show every extreme that they name: `vectors`: eigenvector amplitudes vary over the basis. `tile_rows`: the first tile_counts slots of a term on a device name distinct tiles whose global tile row is at least the global tile column; later slots are ignored. `tile_cols`: see tile_rows. `tile_counts`: loads differ from device to device. `tile_diag`: 1 exactly for live slots whose global tile row equals the global tile column, else 0.
All inputs are finite; a program needn't handle non-finite values.
Results may differ from the reference program's by a relative error of at most 0.0003.
Values may be sent and summed in bfloat16 or wider, within the bound.
A program may use at most 64 MiB of HBM per device.

```python
import math
import jax
import jax.numpy as jnp
from jax import lax

EV = 8
NTERM = 3
TILE = 128
PT = 1
GR = 16
GC = 2
K = 4
N = 4096


def layout_draw(key):
    layout_key = jax.random.fold_in(key, 7)
    first_key = jax.random.fold_in(layout_key, 1)
    second_key = jax.random.fold_in(layout_key, 2)
    row_tiles = GC * PT
    col_tiles = GR * PT
    places = row_tiles * col_tiles
    grid_r = jnp.arange(GR, dtype=jnp.int32)[:, None, None]
    grid_c = jnp.arange(GC, dtype=jnp.int32)[None, :, None]
    position = jnp.arange(places, dtype=jnp.int32)
    local_a = position // col_tiles
    local_b = position % col_tiles
    glob_row = (grid_r * GC + local_a // PT) * PT + local_a % PT
    glob_col = (local_b // PT * GC + grid_c) * PT + local_b % PT
    lower = glob_row >= glob_col
    avail = jnp.sum(lower.astype(jnp.int32), axis=-1)
    peak = jnp.max(avail)
    density = jax.random.randint(first_key, (GR, GC, NTERM), 8, 17, dtype=jnp.int32)
    scaled = jnp.maximum(1, K * avail[:, :, None] * density // (8 * peak))
    counts = jnp.minimum(jnp.minimum(K, avail[:, :, None]), scaled).astype(jnp.int32)
    upper_score = max(1, 2 ** 30 // places)
    scores = jax.random.randint(second_key, (GR, GC, NTERM, places), 0, upper_score, dtype=jnp.int32)
    keyed = jnp.where(lower[:, :, None, :], scores * places + position, 2 ** 30 + position)
    order = jnp.argsort(keyed, axis=-1)[..., :K].astype(jnp.int32)
    rows_sel = order // col_tiles
    cols_sel = order % col_tiles
    live = jnp.arange(K, dtype=jnp.int32)[None, None, None, :] < counts[..., None]
    grid_r4 = jnp.arange(GR, dtype=jnp.int32)[:, None, None, None]
    grid_c4 = jnp.arange(GC, dtype=jnp.int32)[None, :, None, None]
    sel_row = (grid_r4 * GC + rows_sel // PT) * PT + rows_sel % PT
    sel_col = (cols_sel // PT * GC + grid_c4) * PT + cols_sel % PT
    flags = jnp.where(live & (sel_row == sel_col), 1, 0).astype(jnp.int32)
    return (rows_sel, cols_sel, counts, flags)


def draw_tile_rows(key, part):
    return layout_draw(key)[0]


def draw_tile_cols(key, part):
    return layout_draw(key)[1]


def draw_tile_counts(key, part):
    return layout_draw(key)[2]


def draw_tile_diag(key, part):
    return layout_draw(key)[3]


def draw_vectors(key, part):
    total = TILE * PT * GR * GC
    place = jnp.arange(total, dtype=jnp.float32) / total
    base = jnp.clip(jax.random.normal(key, (EV, total), jnp.float32), -4.0, 4.0)
    amplitude = jnp.exp(jnp.log(3.0) * place)
    return (base * amplitude[None, :]).astype(jnp.bfloat16)


def shard_levels(stream_key, shape, cuts, least, high):
    gain = 1.0
    for dim, parts in cuts:
        draws = jax.random.uniform(jax.random.fold_in(jax.random.fold_in(stream_key, 6), dim), (parts,), jnp.float32, least / len(cuts), high / len(cuts))
        gain = gain * jnp.repeat(jnp.exp(draws), shape[dim] // parts).reshape((-1,) + (1,) * (len(shape) - 1 - dim))
    return gain


def normal_values(own_key, dims, deviation, bound, cuts=(), kind=jnp.bfloat16):
    drawn = jax.random.normal(own_key, dims, jnp.float32) * deviation
    if len(cuts) > 0:
        drawn = shard_levels(own_key, dims, cuts, -0.22, 0.18) * drawn
    return jnp.clip(drawn, min=-bound, max=bound).astype(kind)


def setup_inputs(seed: int = 0) -> dict:
    streams_of = jax.random.split(jax.random.key(seed), 7)
    vectors = draw_vectors(jax.random.fold_in(streams_of[6], 71), 0)
    tile_vals = normal_values(streams_of[1], (GR, GC, NTERM, K, TILE, TILE), (64 * K) ** -0.5, 0.375, ((0, 16), (1, 2)))
    tile_rows = draw_tile_rows(jax.random.fold_in(streams_of[6], 71), 0)
    tile_cols = draw_tile_cols(jax.random.fold_in(streams_of[6], 71), 0)
    tile_counts = draw_tile_counts(jax.random.fold_in(streams_of[6], 71), 0)
    tile_diag = draw_tile_diag(jax.random.fold_in(streams_of[6], 71), 0)
    return dict(vectors=vectors, tile_vals=tile_vals, tile_rows=tile_rows, tile_cols=tile_cols, tile_counts=tile_counts, tile_diag=tile_diag)


def reference(vectors, tile_vals, tile_rows, tile_cols, tile_counts, tile_diag):
    values = vectors.astype(jnp.float32)
    segments = values.reshape(EV, N // TILE, TILE)
    applied = jnp.zeros((NTERM, EV, N // TILE, TILE), jnp.float32)
    slot_ids = jnp.arange(K, dtype=jnp.int32)

    def device_step(index, applied):
        grid_r = (index // GC).astype(jnp.int32)
        grid_c = (index % GC).astype(jnp.int32)
        for term_idx in range(NTERM):
            tiles_now = tile_vals[grid_r, grid_c, term_idx].astype(jnp.float32)
            rows_now = tile_rows[grid_r, grid_c, term_idx].astype(jnp.int32)
            cols_now = tile_cols[grid_r, grid_c, term_idx].astype(jnp.int32)
            live_wt = (slot_ids < tile_counts[grid_r, grid_c, term_idx]).astype(jnp.float32)
            mirror_wt = live_wt * (1 - tile_diag[grid_r, grid_c, term_idx]).astype(jnp.float32)
            glob_row = ((grid_r * GC + rows_now // PT) * PT + rows_now % PT).astype(jnp.int32)
            glob_col = ((cols_now // PT * GC + grid_c) * PT + cols_now % PT).astype(jnp.int32)
            forward_terms = jnp.einsum('kij,ekj->eki', tiles_now, segments[:, glob_col], precision=lax.Precision.HIGHEST)
            forward_terms = forward_terms * live_wt[None, :, None]
            mirror_terms = jnp.einsum('kij,eki->ekj', tiles_now, segments[:, glob_row], precision=lax.Precision.HIGHEST)
            mirror_terms = mirror_terms * mirror_wt[None, :, None]
            term_slab = applied[term_idx]
            term_slab = term_slab.at[:, glob_row].add(forward_terms)
            term_slab = term_slab.at[:, glob_col].add(mirror_terms)
            applied = applied.at[term_idx].set(term_slab)
        return applied
    applied = lax.fori_loop(0, GR * GC, device_step, applied)
    applied = applied.reshape(NTERM, EV, N)
    raw = jnp.einsum('ei,tfi->tef', values, applied, precision=lax.Precision.HIGHEST)
    return (applied, raw / math.sqrt(N))
```

```python
import functools
import math

import jax
import jax.numpy as jnp
from jax import lax
from jax.experimental import pallas as pl
from jax.experimental.pallas import tpu as pltpu
from jax.sharding import PartitionSpec as P

MESH = pl.DeviceIdType.MESH
HIGHEST = lax.Precision.HIGHEST
LAST = (((1,), (1,)), ((), ()))


def kernel(
    nr, nc, scale,
    v_ref, w_hbm, rows, cols, counts, diag,
    app_ref, sub_ref,
    w, rowv, colv, mterm, mpart, mrecv, fpart, frecv, ssend, srecv,
    w_sem, rv_send, rv_recv, cv_send, cv_recv, m_send, m_recv, f_send, f_recv, s_send, s_recv,
):
    r = lax.axis_index("row")
    c = lax.axis_index("col")
    ev, width = v_ref.shape
    terms, slots = w.shape[0], w.shape[1]
    top = terms * ev

    def remote(src, dst, send, recv, row, col):
        return pltpu.make_async_remote_copy(
            src_ref=src, dst_ref=dst, send_sem=send, recv_sem=recv,
            device_id=(row, col), device_id_type=MESH,
        )

    def each_row(fn):
        @pl.loop(1, nr)
        def _(d):
            fn(lax.rem(r + d, nr))

    def each_col(fn):
        @pl.loop(1, nc)
        def _(d):
            fn(lax.rem(c + d, nc))

    w_copy = pltpu.make_async_copy(w_hbm.at[0, 0], w, w_sem)
    w_copy.start()

    barrier = pltpu.get_barrier_semaphore()
    each_row(lambda p: pl.semaphore_signal(barrier, inc=1, device_id=(p, c), device_id_type=MESH))
    each_col(lambda p: pl.semaphore_signal(barrier, inc=1, device_id=(r, p), device_id_type=MESH))
    own = v_ref[...]
    rowv[c] = own
    colv[r] = own

    @pl.loop(r + 1, nr)
    def _(b):
        colv[b] = jnp.zeros_like(own)

    pl.semaphore_wait(barrier, nr - 1 + nc - 1)

    def rv(p):
        return remote(v_ref, rowv.at[c], rv_send.at[p], rv_recv.at[c], r, p)

    def cv(p):
        return remote(v_ref, colv.at[r], cv_send.at[p], cv_recv.at[r], p, c)

    each_col(lambda p: rv(p).start())

    @pl.loop(0, nr - 1 - r)
    def _(i):
        cv(nr - 1 - i).start()

    w_copy.wait()
    each_col(lambda p: remote(v_ref, rowv.at[p], rv_send.at[p], rv_recv.at[p], r, p).wait_recv())

    live = []
    off = []
    for t in range(terms):
        for k in range(slots):
            alive = k < counts[0, 0, t]
            live.append(jnp.where(alive, 1.0, 0.0).astype(jnp.float32))
            off.append(jnp.where(alive & (diag[0, t, 0, k] == 0), 1.0, 0.0).astype(jnp.float32))
            mterm[t, k] = jnp.dot(
                rowv[rows[0, t, 0, k]], w[t, k], preferred_element_type=jnp.float32
            )

    @pl.loop(0, r + 1)
    def _(b):
        for t in range(terms):
            total = jnp.zeros((ev, width), jnp.float32)
            for k in range(slots):
                weight = jnp.where(cols[0, t, 0, k] == b, off[t * slots + k], 0.0)
                total += weight * mterm[t, k]
            mpart[b, t] = total

    def mp(b):
        return remote(mpart.at[b], mrecv.at[r], m_send.at[b], m_recv.at[r], b, c)

    @pl.loop(0, r)
    def _(b):
        mp(b).start()

    @pl.loop(0, r)
    def _(b):
        remote(v_ref, colv.at[b], cv_send.at[b], cv_recv.at[b], b, c).wait_recv()

    forward = []
    small = []
    for t in range(terms):
        seen = []
        for k in range(slots):
            seen.append(colv[jnp.minimum(cols[0, t, 0, k], r)])
            forward.append(
                lax.dot_general(seen[k], w[t, k], LAST, preferred_element_type=jnp.float32)
                * live[t * slots + k]
            )
        wide = jnp.concatenate(seen, axis=1).astype(jnp.float32)
        ahead = jnp.concatenate([mterm[t, k] * live[t * slots + k] for k in range(slots)], axis=1)
        back = jnp.concatenate([mterm[t, k] * off[t * slots + k] for k in range(slots)], axis=1)
        small.append(
            lax.dot_general(ahead, wide, LAST, precision=HIGHEST, preferred_element_type=jnp.float32)
            + lax.dot_general(wide, back, LAST, precision=HIGHEST, preferred_element_type=jnp.float32)
        )
    small.append(jnp.zeros((ev, width - top), jnp.float32))
    packed = jnp.concatenate(small, axis=1)
    for a in range(nc):
        for t in range(terms):
            total = jnp.zeros((ev, width), jnp.float32)
            for k in range(slots):
                total += jnp.where(rows[0, t, 0, k] == a, 1.0, 0.0) * forward[t * slots + k]
            fpart[a, t] = total
        fpart[a, terms] = packed

    def fp(p):
        return remote(fpart.at[p], frecv.at[c], f_send.at[p], f_recv.at[c], r, p)

    each_col(lambda p: fp(p).start())
    frecv[c] = fpart[c]
    each_col(
        lambda p: remote(fpart.at[p], frecv.at[p], f_send.at[p], f_recv.at[p], r, p).wait_recv()
    )
    sums = frecv[0]
    for a in range(1, nc):
        sums += frecv[a]
    ssend[...] = sums[terms]
    srecv[r] = sums[terms]

    def sp(p):
        return remote(ssend, srecv.at[r], s_send.at[p], s_recv.at[r], p, c)

    each_row(lambda p: sp(p).start())

    app_ref[...] = sums[:terms] + mpart[r]

    @pl.loop(0, nr - 1 - r)
    def _(i):
        s = r + 1 + i
        remote(mpart.at[s], mrecv.at[s], m_send.at[s], m_recv.at[s], s, c).wait_recv()
        app_ref[...] += mrecv[s]

    each_row(lambda p: remote(ssend, srecv.at[p], s_send.at[p], s_recv.at[p], p, c).wait_recv())
    whole = srecv[0]
    for s in range(1, nr):
        whole += srecv[s]
    for t in range(terms):
        sub_ref[t] = whole[:, t * ev : (t + 1) * ev] * scale

    each_col(lambda p: rv(p).wait_send())
    each_col(lambda p: fp(p).wait_send())
    each_row(lambda p: sp(p).wait_send())

    @pl.loop(0, nr - 1 - r)
    def _(i):
        cv(nr - 1 - i).wait_send()

    @pl.loop(0, r)
    def _(b):
        mp(b).wait_send()


def flip(table):
    return jnp.swapaxes(table, 1, 2)


def shards(nr, nc, vectors, tile_vals, tile_rows, tile_cols, tile_counts, tile_diag):
    ev, width = vectors.shape
    terms, slots = tile_vals.shape[2], tile_vals.shape[3]
    f32 = jnp.float32
    scale = 1.0 / math.sqrt(width * nr * nc)
    vmem = pl.BlockSpec(memory_space=pltpu.VMEM)
    smem = pl.BlockSpec(memory_space=pltpu.SMEM)
    dma = pltpu.SemaphoreType.DMA
    return pl.pallas_call(
        functools.partial(kernel, nr, nc, scale),
        out_shape=(
            jax.ShapeDtypeStruct((terms, ev, width), f32),
            jax.ShapeDtypeStruct((terms, ev, ev), f32),
        ),
        in_specs=[vmem, pl.BlockSpec(memory_space=pl.ANY), smem, smem, smem, smem],
        out_specs=(vmem, vmem),
        scratch_shapes=[
            pltpu.VMEM(tile_vals.shape[2:], tile_vals.dtype),
            pltpu.VMEM((nc, ev, width), vectors.dtype),
            pltpu.VMEM((nr, ev, width), vectors.dtype),
            pltpu.VMEM((terms, slots, ev, width), f32),
            pltpu.VMEM((nr, terms, ev, width), f32),
            pltpu.VMEM((nr, terms, ev, width), f32),
            pltpu.VMEM((nc, terms + 1, ev, width), f32),
            pltpu.VMEM((nc, terms + 1, ev, width), f32),
            pltpu.VMEM((ev, width), f32),
            pltpu.VMEM((nr, ev, width), f32),
            dma,
            dma((nc,)), dma((nc,)), dma((nr,)), dma((nr,)), dma((nr,)), dma((nr,)),
            dma((nc,)), dma((nc,)), dma((nr,)), dma((nr,)),
        ],
        compiler_params=pltpu.CompilerParams(collective_id=0, has_side_effects=True),
    )(vectors, tile_vals, flip(tile_rows), flip(tile_cols), tile_counts, flip(tile_diag))


def solution(mesh):
    placed = (
        P(None, ("row", "col")),
        P("row", "col", None, None, None, None),
        P("row", "col", None, None),
        P("row", "col", None, None),
        P("row", "col", None),
        P("row", "col", None, None),
    )
    return jax.shard_map(
        functools.partial(shards, mesh.shape["row"], mesh.shape["col"]),
        mesh=mesh,
        in_specs=placed,
        out_specs=(P(None, None, ("row", "col")), P()),
        check_vma=False,
    )
```

```python
import functools
import math

import jax
import jax.numpy as jnp
from jax import lax
from jax.experimental import pallas as pl
from jax.experimental.pallas import tpu as pltpu
from jax.sharding import PartitionSpec as P

MESH = pl.DeviceIdType.MESH
HIGHEST = lax.Precision.HIGHEST
LAST = (((1,), (1,)), ((), ()))


def kernel(
    nr, nc, scale,
    v_ref, w_hbm, rows, cols, counts, diag,
    app_ref, sub_ref,
    w, rowv, colv, mterm, mpart, pair, msum, mrecv, fpart, frecv, ssend, srecv,
    w_sem, rv_send, rv_recv, cv_send, cv_recv, p_send, p_recv, m_send, m_recv, f_send, f_recv, s_send, s_recv,
):
    r = lax.axis_index("row")
    c = lax.axis_index("col")
    q = r // 2
    half = lax.rem(r, 2)
    ev, width = v_ref.shape
    terms, slots = w.shape[0], w.shape[1]
    top = terms * ev

    def remote(src, dst, send, recv, row, col):
        return pltpu.make_async_remote_copy(
            src_ref=src, dst_ref=dst, send_sem=send, recv_sem=recv,
            device_id=(row, col), device_id_type=MESH,
        )

    def each_row(fn):
        @pl.loop(1, nr)
        def _(d):
            fn(lax.rem(r + d, nr))

    def each_col(fn):
        @pl.loop(1, nc)
        def _(d):
            fn(lax.rem(c + d, nc))

    w_copy = pltpu.make_async_copy(w_hbm.at[0, 0], w, w_sem)
    w_copy.start()

    live = []
    off = []
    for t in range(terms):
        for k in range(slots):
            alive = k < counts[0, 0, t]
            live.append(jnp.where(alive, 1.0, 0.0).astype(jnp.float32))
            off.append(jnp.where(alive & (diag[0, t, 0, k] == 0), 1.0, 0.0).astype(jnp.float32))

    barrier = pltpu.get_barrier_semaphore()
    each_row(lambda p: pl.semaphore_signal(barrier, inc=1, device_id=(p, c), device_id_type=MESH))
    each_col(lambda p: pl.semaphore_signal(barrier, inc=1, device_id=(r, p), device_id_type=MESH))
    own = v_ref[...]
    rowv[c] = own
    colv[r] = own

    @pl.loop(r + 1, nr)
    def _(b):
        colv[b] = jnp.zeros_like(own)

    pl.semaphore_wait(barrier, nr - 1 + nc - 1)

    def rv(p):
        return remote(v_ref, rowv.at[c], rv_send.at[p], rv_recv.at[c], r, p)

    def cv(p):
        return remote(v_ref, colv.at[r], cv_send.at[p], cv_recv.at[r], p, c)

    each_col(lambda p: rv(p).start())

    @pl.loop(0, nr - 1 - r)
    def _(i):
        cv(nr - 1 - i).start()

    w_copy.wait()
    each_col(lambda p: remote(v_ref, rowv.at[p], rv_send.at[p], rv_recv.at[p], r, p).wait_recv())

    for t in range(terms):
        for k in range(slots):
            mterm[t, k] = jnp.dot(
                rowv[rows[0, t, 0, k]], w[t, k], preferred_element_type=jnp.float32
            )

    def place(side, j):
        b = 2 * j + side
        for t in range(terms):
            total = jnp.zeros((ev, width), jnp.float32)
            for k in range(slots):
                weight = jnp.where(cols[0, t, 0, k] == b, off[t * slots + k], 0.0)
                total += weight * mterm[t, k]
            mpart[side, j, t] = total

    def pp(j):
        return remote(
            mpart.at[1 - half, j], pair.at[j], p_send.at[j], p_recv.at[j], r + 1 - 2 * half, c
        )

    place(1 - half, 0)

    @pl.loop(1, q + 1)
    def _(j):
        place(1 - half, j)
        pp(j - 1).start()

    pp(q).start()

    @pl.loop(0, q + 1)
    def _(j):
        place(half, j)

    def mp(j):
        return remote(
            msum.at[j], mrecv.at[q], m_send.at[j], m_recv.at[q], 2 * j + half, c
        )

    pp(0).wait_recv()
    msum[0] = mpart[half, 0] + pair[0]

    @pl.loop(1, q + 1)
    def _(j):
        pp(j).wait_recv()
        msum[j] = mpart[half, j] + pair[j]
        mp(j - 1).start()

    @pl.loop(0, r)
    def _(b):
        remote(v_ref, colv.at[b], cv_send.at[b], cv_recv.at[b], b, c).wait_recv()

    forward = []
    small = []
    for t in range(terms):
        seen = []
        for k in range(slots):
            seen.append(colv[jnp.minimum(cols[0, t, 0, k], r)])
            forward.append(
                lax.dot_general(seen[k], w[t, k], LAST, preferred_element_type=jnp.float32)
                * live[t * slots + k]
            )
        wide = jnp.concatenate(seen, axis=1).astype(jnp.float32)
        ahead = jnp.concatenate([mterm[t, k] * live[t * slots + k] for k in range(slots)], axis=1)
        back = jnp.concatenate([mterm[t, k] * off[t * slots + k] for k in range(slots)], axis=1)
        small.append(
            lax.dot_general(ahead, wide, LAST, precision=HIGHEST, preferred_element_type=jnp.float32)
            + lax.dot_general(wide, back, LAST, precision=HIGHEST, preferred_element_type=jnp.float32)
        )
    small.append(jnp.zeros((ev, width - top), jnp.float32))
    packed = jnp.concatenate(small, axis=1)
    for a in range(nc):
        for t in range(terms):
            total = jnp.zeros((ev, width), jnp.float32)
            for k in range(slots):
                total += jnp.where(rows[0, t, 0, k] == a, 1.0, 0.0) * forward[t * slots + k]
            fpart[a, t] = total
        fpart[a, terms] = packed

    def fp(p):
        return remote(fpart.at[p], frecv.at[c], f_send.at[p], f_recv.at[c], r, p)

    each_col(lambda p: fp(p).start())
    frecv[c] = fpart[c]
    each_col(
        lambda p: remote(fpart.at[p], frecv.at[p], f_send.at[p], f_recv.at[p], r, p).wait_recv()
    )
    sums = frecv[0]
    for a in range(1, nc):
        sums += frecv[a]
    ssend[...] = sums[terms]
    srecv[r] = sums[terms]

    def sp(p):
        return remote(ssend, srecv.at[r], s_send.at[p], s_recv.at[r], p, c)

    each_row(lambda p: sp(p).start())

    app_ref[...] = sums[:terms] + msum[q]

    @pl.loop(q + 1, nr // 2)
    def _(s):
        remote(
            msum.at[s], mrecv.at[s], m_send.at[s], m_recv.at[s], 2 * s + half, c
        ).wait_recv()
        app_ref[...] += mrecv[s]

    each_row(lambda p: remote(ssend, srecv.at[p], s_send.at[p], s_recv.at[p], p, c).wait_recv())
    whole = srecv[0]
    for s in range(1, nr):
        whole += srecv[s]
    for t in range(terms):
        sub_ref[t] = whole[:, t * ev : (t + 1) * ev] * scale

    each_col(lambda p: rv(p).wait_send())
    each_col(lambda p: fp(p).wait_send())
    each_row(lambda p: sp(p).wait_send())

    @pl.loop(0, nr - 1 - r)
    def _(i):
        cv(nr - 1 - i).wait_send()

    @pl.loop(0, q + 1)
    def _(j):
        pp(j).wait_send()

    @pl.loop(0, q)
    def _(j):
        mp(j).wait_send()


def flip(table):
    return jnp.swapaxes(table, 1, 2)


def shards(nr, nc, vectors, tile_vals, tile_rows, tile_cols, tile_counts, tile_diag):
    ev, width = vectors.shape
    terms, slots = tile_vals.shape[2], tile_vals.shape[3]
    f32 = jnp.float32
    scale = 1.0 / math.sqrt(width * nr * nc)
    vmem = pl.BlockSpec(memory_space=pltpu.VMEM)
    smem = pl.BlockSpec(memory_space=pltpu.SMEM)
    dma = pltpu.SemaphoreType.DMA
    return pl.pallas_call(
        functools.partial(kernel, nr, nc, scale),
        out_shape=(
            jax.ShapeDtypeStruct((terms, ev, width), f32),
            jax.ShapeDtypeStruct((terms, ev, ev), f32),
        ),
        in_specs=[vmem, pl.BlockSpec(memory_space=pl.ANY), smem, smem, smem, smem],
        out_specs=(vmem, vmem),
        scratch_shapes=[
            pltpu.VMEM(tile_vals.shape[2:], tile_vals.dtype),
            pltpu.VMEM((nc, ev, width), vectors.dtype),
            pltpu.VMEM((nr, ev, width), vectors.dtype),
            pltpu.VMEM((terms, slots, ev, width), f32),
            pltpu.VMEM((2, nr // 2, terms, ev, width), f32),
            pltpu.VMEM((nr // 2, terms, ev, width), f32),
            pltpu.VMEM((nr // 2, terms, ev, width), f32),
            pltpu.VMEM((nr // 2, terms, ev, width), f32),
            pltpu.VMEM((nc, terms + 1, ev, width), f32),
            pltpu.VMEM((nc, terms + 1, ev, width), f32),
            pltpu.VMEM((ev, width), f32),
            pltpu.VMEM((nr, ev, width), f32),
            dma,
            dma((nc,)), dma((nc,)), dma((nr,)), dma((nr,)),
            dma((nr // 2,)), dma((nr // 2,)), dma((nr // 2,)), dma((nr // 2,)),
            dma((nc,)), dma((nc,)), dma((nr,)), dma((nr,)),
        ],
        compiler_params=pltpu.CompilerParams(collective_id=0, has_side_effects=True),
    )(vectors, tile_vals, flip(tile_rows), flip(tile_cols), tile_counts, flip(tile_diag))


def solution(mesh):
    placed = (
        P(None, ("row", "col")),
        P("row", "col", None, None, None, None),
        P("row", "col", None, None),
        P("row", "col", None, None),
        P("row", "col", None),
        P("row", "col", None, None),
    )
    return jax.shard_map(
        functools.partial(shards, mesh.shape["row"], mesh.shape["col"]),
        mesh=mesh,
        in_specs=placed,
        out_specs=(P(None, None, ("row", "col")), P()),
        check_vma=False,
    )
```

```python
import functools
import math

import jax
import jax.numpy as jnp
from jax import lax
from jax.experimental import pallas as pl
from jax.experimental.pallas import tpu as pltpu
from jax.sharding import PartitionSpec as P

MESH = pl.DeviceIdType.MESH
LAST = (((1,), (1,)), ((), ()))


def kernel(
    nr, nc, scale,
    v_hbm, w_hbm, rows_hbm, cols_hbm, counts_hbm, diag_hbm,
    app_ref, sub_ref,
    v_ref, rows, cols, counts, diag,
    w, rowv, colv, mterm, ahead, back, mpart, pair, msum, mrecv, fpart, frecv, yrecv, ssend, srecv,
    in_sem, w_sem, rv_send, rv_recv, cv_send, cv_recv, p_send, p_recv, m_send, m_recv,
    f_send, f_recv, y_send, y_recv, s_send, s_recv,
):
    r = lax.axis_index("row")
    c = lax.axis_index("col")
    q = r // 2
    half = lax.rem(r, 2)
    ev, width = v_ref.shape
    terms, slots = w.shape[0], w.shape[1]
    top = terms * ev

    def remote(src, dst, send, recv, row, col):
        return pltpu.make_async_remote_copy(
            src_ref=src, dst_ref=dst, send_sem=send, recv_sem=recv,
            device_id=(row, col), device_id_type=MESH,
        )

    def each_row(fn):
        @pl.loop(1, nr)
        def _(d):
            fn(lax.rem(r + d, nr))

    def each_col(fn):
        @pl.loop(1, nc)
        def _(d):
            fn(lax.rem(c + d, nc))

    barrier = pltpu.get_barrier_semaphore()
    each_row(lambda p: pl.semaphore_signal(barrier, inc=1, device_id=(p, c), device_id_type=MESH))
    each_col(lambda p: pl.semaphore_signal(barrier, inc=1, device_id=(r, p), device_id_type=MESH))

    small_in = [
        pltpu.make_async_copy(src, dst, in_sem.at[i])
        for i, (src, dst) in enumerate(
            [(v_hbm, v_ref), (rows_hbm, rows), (cols_hbm, cols), (counts_hbm, counts), (diag_hbm, diag)]
        )
    ]
    for copy in small_in:
        copy.start()
    w_copy = pltpu.make_async_copy(w_hbm.at[0, 0], w, w_sem)
    w_copy.start()
    zero = jnp.zeros((ev, width), v_ref.dtype)

    @pl.loop(r + 1, nr)
    def _(b):
        colv[b] = zero

    for copy in small_in:
        copy.wait()
    own = v_ref[...]
    rowv[c] = own
    colv[r] = own
    live = []
    off = []
    for t in range(terms):
        for k in range(slots):
            alive = k < counts[0, 0, t]
            live.append(jnp.where(alive, 1.0, 0.0).astype(jnp.float32))
            off.append(jnp.where(alive & (diag[0, t, 0, k] == 0), 1.0, 0.0).astype(jnp.float32))
    pl.semaphore_wait(barrier, nr - 1 + nc - 1)

    def rv(p):
        return remote(v_ref, rowv.at[c], rv_send.at[p], rv_recv.at[c], r, p)

    def cv(p):
        return remote(v_ref, colv.at[r], cv_send.at[p], cv_recv.at[r], p, c)

    each_col(lambda p: rv(p).start())

    @pl.loop(0, nr - 1 - r)
    def _(i):
        cv(nr - 1 - i).start()

    w_copy.wait()
    each_col(lambda p: remote(v_ref, rowv.at[p], rv_send.at[p], rv_recv.at[p], r, p).wait_recv())

    for t in range(terms):
        for k in range(slots):
            mterm[t, k] = jnp.dot(
                rowv[rows[0, t, 0, k]], w[t, k], preferred_element_type=jnp.float32
            )

    def place(side, j):
        b = 2 * j + side
        for t in range(terms):
            total = jnp.zeros((ev, width), jnp.float32)
            for k in range(slots):
                weight = jnp.where(cols[0, t, 0, k] == b, off[t * slots + k], 0.0)
                total += weight * mterm[t, k]
            mpart[side, j, t] = total

    def pp(j):
        return remote(
            mpart.at[1 - half, j], pair.at[j], p_send.at[j], p_recv.at[j], r + 1 - 2 * half, c
        )

    place(1 - half, 0)

    @pl.loop(1, q + 1)
    def _(j):
        place(1 - half, j)
        pp(j - 1).start()

    pp(q).start()

    @pl.loop(0, q + 1)
    def _(j):
        place(half, j)

    def parts(value):
        high = value.astype(jnp.bfloat16)
        rest = value - high.astype(jnp.float32)
        middle = rest.astype(jnp.bfloat16)
        low = (rest - middle.astype(jnp.float32)).astype(jnp.bfloat16)
        return jnp.concatenate([high, middle, low], axis=0)

    for t in range(terms):
        for k in range(slots):
            lanes = pl.ds(k * width, width)
            split = parts(mterm[t, k])
            ahead[t, :, lanes] = split * live[t * slots + k].astype(jnp.bfloat16)
            back[t, :, lanes] = split * off[t * slots + k].astype(jnp.bfloat16)

    @pl.loop(0, r)
    def _(b):
        remote(v_ref, colv.at[b], cv_send.at[b], cv_recv.at[b], b, c).wait_recv()

    small = []
    for t in range(terms):
        wide = jnp.concatenate(
            [colv[jnp.minimum(cols[0, t, 0, k], r)] for k in range(slots)], axis=1
        )
        one = lax.dot_general(ahead[t], wide, LAST, preferred_element_type=jnp.float32)
        two = lax.dot_general(wide, back[t], LAST, preferred_element_type=jnp.float32)
        small.append(
            (one[2 * ev :] + one[ev : 2 * ev]) + one[:ev]
            + ((two[:, 2 * ev :] + two[:, ev : 2 * ev]) + two[:, :ev])
        )
    small.append(jnp.zeros((ev, width - top), jnp.float32))
    packed = jnp.concatenate(small, axis=1)

    per = width // top
    lines = -(-ev // per)
    line = lax.broadcasted_iota(jnp.int32, (ev, width), 0)
    group = lax.broadcasted_iota(jnp.int32, (ev, width), 1) // top
    spread = packed
    for g in range(1, per):
        spread += pltpu.roll(packed, g * top, 1)
    for n in range(lines):
        picked = jnp.where(line == group + n * per, jnp.where(group < per, spread, 0.0), 0.0)
        ssend[0, n] = jnp.sum(picked, axis=0)

    def yp(p):
        return remote(ssend.at[0], yrecv.at[c], y_send.at[p], y_recv.at[c], r, p)

    each_col(lambda p: yp(p).start())
    yrecv[c] = ssend[0]

    for t in range(terms):
        totals = [jnp.zeros((ev, width), jnp.float32) for _ in range(nc)]
        for k in range(slots):
            seen = colv[jnp.minimum(cols[0, t, 0, k], r)]
            moved = lax.dot_general(seen, w[t, k], LAST, preferred_element_type=jnp.float32)
            for a in range(nc):
                weight = jnp.where(rows[0, t, 0, k] == a, live[t * slots + k], 0.0)
                totals[a] += weight * moved
        for a in range(nc):
            fpart[a, t] = totals[a]

    def fp(p):
        return remote(fpart.at[p], frecv.at[c], f_send.at[p], f_recv.at[c], r, p)

    each_col(lambda p: fp(p).start())
    frecv[c] = fpart[c]

    def mp(j):
        return remote(
            msum.at[j], mrecv.at[q], m_send.at[j], m_recv.at[q], 2 * j + half, c
        )

    pp(0).wait_recv()
    msum[0] = mpart[half, 0] + pair[0]

    @pl.loop(1, q + 1)
    def _(j):
        pp(j).wait_recv()
        msum[j] = mpart[half, j] + pair[j]
        mp(j - 1).start()

    each_col(
        lambda p: remote(ssend.at[0], yrecv.at[p], y_send.at[p], y_recv.at[p], r, p).wait_recv()
    )
    level = yrecv[0]
    for a in range(1, nc):
        level += yrecv[a]
    ssend[1] = level
    srecv[r] = level

    def sp(p):
        return remote(ssend.at[1], srecv.at[r], s_send.at[p], s_recv.at[r], p, c)

    each_row(lambda p: sp(p).start())

    each_col(
        lambda p: remote(fpart.at[p], frecv.at[p], f_send.at[p], f_recv.at[p], r, p).wait_recv()
    )
    sums = frecv[0]
    for a in range(1, nc):
        sums += frecv[a]
    app_ref[...] = sums + msum[q]

    @pl.loop(q + 1, nr // 2)
    def _(s):
        remote(
            msum.at[s], mrecv.at[s], m_send.at[s], m_recv.at[s], 2 * s + half, c
        ).wait_recv()
        app_ref[...] += mrecv[s]

    each_row(
        lambda p: remote(ssend.at[1], srecv.at[p], s_send.at[p], s_recv.at[p], p, c).wait_recv()
    )
    whole = srecv[0]
    for s in range(1, nr):
        whole += srecv[s]
    picked = jnp.zeros((ev, width), jnp.float32)
    for n in range(lines):
        picked += jnp.where(
            line == group + n * per,
            jnp.where(group < per, jnp.broadcast_to(whole[n : n + 1], (ev, width)), 0.0),
            0.0,
        )
    spread = picked
    for g in range(1, per):
        spread += pltpu.roll(picked, width - g * top, 1)
    for t in range(terms):
        sub_ref[t] = spread[:, t * ev : (t + 1) * ev] * scale

    each_col(lambda p: yp(p).wait_send())
    each_col(lambda p: rv(p).wait_send())
    each_col(lambda p: fp(p).wait_send())
    each_row(lambda p: sp(p).wait_send())

    @pl.loop(0, nr - 1 - r)
    def _(i):
        cv(nr - 1 - i).wait_send()

    @pl.loop(0, q + 1)
    def _(j):
        pp(j).wait_send()

    @pl.loop(0, q)
    def _(j):
        mp(j).wait_send()


def flip(table):
    return jnp.swapaxes(table, 1, 2)


def shards(nr, nc, vectors, tile_vals, tile_rows, tile_cols, tile_counts, tile_diag):
    ev, width = vectors.shape
    terms, slots = tile_vals.shape[2], tile_vals.shape[3]
    f32 = jnp.float32
    scale = 1.0 / math.sqrt(width * nr * nc)
    vmem = pl.BlockSpec(memory_space=pltpu.VMEM)
    top = terms * ev
    lines = -(-ev // (width // top))
    table = pltpu.SMEM((1, terms, 1, slots), jnp.int32)
    dma = pltpu.SemaphoreType.DMA
    return pl.pallas_call(
        functools.partial(kernel, nr, nc, scale),
        out_shape=(
            jax.ShapeDtypeStruct((terms, ev, width), f32),
            jax.ShapeDtypeStruct((terms, ev, ev), f32),
        ),
        in_specs=[pl.BlockSpec(memory_space=pl.ANY)] * 6,
        out_specs=(vmem, vmem),
        scratch_shapes=[
            pltpu.VMEM(vectors.shape, vectors.dtype),
            table, table, pltpu.SMEM(tile_counts.shape, jnp.int32), table,
            pltpu.VMEM(tile_vals.shape[2:], tile_vals.dtype),
            pltpu.VMEM((nc, ev, width), vectors.dtype),
            pltpu.VMEM((nr, ev, width), vectors.dtype),
            pltpu.VMEM((terms, slots, ev, width), f32),
            pltpu.VMEM((terms, 3 * ev, slots * width), jnp.bfloat16),
            pltpu.VMEM((terms, 3 * ev, slots * width), jnp.bfloat16),
            pltpu.VMEM((2, nr // 2, terms, ev, width), f32),
            pltpu.VMEM((nr // 2, terms, ev, width), f32),
            pltpu.VMEM((nr // 2, terms, ev, width), f32),
            pltpu.VMEM((nr // 2, terms, ev, width), f32),
            pltpu.VMEM((nc, terms, ev, width), f32),
            pltpu.VMEM((nc, terms, ev, width), f32),
            pltpu.VMEM((nc, lines, width), f32),
            pltpu.VMEM((2, lines, width), f32),
            pltpu.VMEM((nr, lines, width), f32),
            dma((5,)), dma,
            dma((nc,)), dma((nc,)), dma((nr,)), dma((nr,)),
            dma((nr // 2,)), dma((nr // 2,)), dma((nr // 2,)), dma((nr // 2,)),
            dma((nc,)), dma((nc,)), dma((nc,)), dma((nc,)), dma((nr,)), dma((nr,)),
        ],
        compiler_params=pltpu.CompilerParams(collective_id=0, has_side_effects=True),
    )(vectors, tile_vals, flip(tile_rows), flip(tile_cols), tile_counts, flip(tile_diag))


def solution(mesh):
    placed = (
        P(None, ("row", "col")),
        P("row", "col", None, None, None, None),
        P("row", "col", None, None),
        P("row", "col", None, None),
        P("row", "col", None),
        P("row", "col", None, None),
    )
    return jax.shard_map(
        functools.partial(shards, mesh.shape["row"], mesh.shape["col"]),
        mesh=mesh,
        in_specs=placed,
        out_specs=(P(None, None, ("row", "col")), P()),
        check_vma=False,
    )
```

```python
import functools
import math

import jax
import jax.numpy as jnp
from jax import lax
from jax.experimental import pallas as pl
from jax.experimental.pallas import tpu as pltpu
from jax.sharding import PartitionSpec as P

LIMIT = 16 * 2**20
MESH = pl.DeviceIdType.MESH
LAST = (((1,), (1,)), ((), ()))


def kernel(
    nr, nc, scale,
    v_hbm, w_hbm, rows_hbm, cols_hbm, counts_hbm, diag_hbm,
    app_ref, sub_ref,
    v_ref, rows, cols, counts, diag,
    w, rowv, colv, mterm, ahead, back, mpart, pair, msum, mrecv, fpart, frecv, ssend, srecv,
    in_sem, w_sem, rv_send, rv_recv, cv_send, cv_recv, p_send, p_recv, m_send, m_recv,
    f_send, f_recv, s_send, s_recv,
):
    r = lax.axis_index("row")
    c = lax.axis_index("col")
    q = r // 2
    half = lax.rem(r, 2)
    ev, width = v_ref.shape
    terms, slots = w.shape[0], w.shape[1]
    top = terms * ev

    def remote(src, dst, send, recv, row, col):
        return pltpu.make_async_remote_copy(
            src_ref=src, dst_ref=dst, send_sem=send, recv_sem=recv,
            device_id=(row, col), device_id_type=MESH,
        )

    def each_row(fn):
        @pl.loop(1, nr)
        def _(d):
            fn(lax.rem(r + d, nr))

    def each_col(fn):
        @pl.loop(1, nc)
        def _(d):
            fn(lax.rem(c + d, nc))

    barrier = pltpu.get_barrier_semaphore()
    each_row(lambda p: pl.semaphore_signal(barrier, inc=1, device_id=(p, c), device_id_type=MESH))
    each_col(lambda p: pl.semaphore_signal(barrier, inc=1, device_id=(r, p), device_id_type=MESH))

    small_in = [
        pltpu.make_async_copy(src, dst, in_sem.at[i])
        for i, (src, dst) in enumerate(
            [(v_hbm, v_ref), (rows_hbm, rows), (cols_hbm, cols), (counts_hbm, counts), (diag_hbm, diag)]
        )
    ]
    for copy in small_in:
        copy.start()
    w_copy = pltpu.make_async_copy(w_hbm.at[0, 0], w, w_sem)
    w_copy.start()
    zero = jnp.zeros((ev, width), v_ref.dtype)

    @pl.loop(r + 1, nr)
    def _(b):
        colv[b] = zero

    for copy in small_in:
        copy.wait()
    own = v_ref[...]
    rowv[c] = own
    colv[r] = own
    live = []
    off = []
    for t in range(terms):
        for k in range(slots):
            alive = k < counts[0, 0, t]
            live.append(jnp.where(alive, 1.0, 0.0).astype(jnp.float32))
            off.append(jnp.where(alive & (diag[0, t, 0, k] == 0), 1.0, 0.0).astype(jnp.float32))
    pl.semaphore_wait(barrier, nr - 1 + nc - 1)

    def rv(p):
        return remote(v_ref, rowv.at[c], rv_send.at[p], rv_recv.at[c], r, p)

    def cv(p):
        return remote(v_ref, colv.at[r], cv_send.at[p], cv_recv.at[r], p, c)

    each_col(lambda p: rv(p).start())

    @pl.loop(0, nr - 1 - r)
    def _(i):
        cv(nr - 1 - i).start()

    w_copy.wait()
    each_col(lambda p: remote(v_ref, rowv.at[p], rv_send.at[p], rv_recv.at[p], r, p).wait_recv())

    for t in range(terms):
        for k in range(slots):
            mterm[t, k] = jnp.dot(
                rowv[rows[0, t, 0, k]], w[t, k], preferred_element_type=jnp.float32
            )

    def place(side, j):
        b = 2 * j + side
        for t in range(terms):
            total = jnp.zeros((ev, width), jnp.float32)
            for k in range(slots):
                weight = jnp.where(cols[0, t, 0, k] == b, off[t * slots + k], 0.0)
                total += weight * mterm[t, k]
            mpart[side, j, t] = total

    def pp(j):
        return remote(
            mpart.at[1 - half, j], pair.at[j], p_send.at[j], p_recv.at[j], r + 1 - 2 * half, c
        )

    place(1 - half, 0)

    @pl.loop(1, q + 1)
    def _(j):
        place(1 - half, j)
        pp(j - 1).start()

    pp(q).start()

    @pl.loop(0, q + 1)
    def _(j):
        place(half, j)

    def parts(value):
        high = value.astype(jnp.bfloat16)
        rest = value - high.astype(jnp.float32)
        middle = rest.astype(jnp.bfloat16)
        low = (rest - middle.astype(jnp.float32)).astype(jnp.bfloat16)
        return jnp.concatenate([high, middle, low], axis=0)

    for t in range(terms):
        for k in range(slots):
            lanes = pl.ds(k * width, width)
            split = parts(mterm[t, k])
            ahead[t, :, lanes] = split * live[t * slots + k].astype(jnp.bfloat16)
            back[t, :, lanes] = split * off[t * slots + k].astype(jnp.bfloat16)

    @pl.loop(0, r)
    def _(b):
        remote(v_ref, colv.at[b], cv_send.at[b], cv_recv.at[b], b, c).wait_recv()

    small = []
    for t in range(terms):
        wide = jnp.concatenate(
            [colv[jnp.minimum(cols[0, t, 0, k], r)] for k in range(slots)], axis=1
        )
        one = lax.dot_general(ahead[t], wide, LAST, preferred_element_type=jnp.float32)
        two = lax.dot_general(wide, back[t], LAST, preferred_element_type=jnp.float32)
        small.append(
            (one[2 * ev :] + one[ev : 2 * ev]) + one[:ev]
            + ((two[:, 2 * ev :] + two[:, ev : 2 * ev]) + two[:, :ev])
        )
    small.append(jnp.zeros((ev, width - top), jnp.float32))
    packed = jnp.concatenate(small, axis=1)

    per = width // top
    lines = -(-ev // per)
    line = lax.broadcasted_iota(jnp.int32, (ev, width), 0)
    group = lax.broadcasted_iota(jnp.int32, (ev, width), 1) // top
    spread = packed
    for g in range(1, per):
        spread += pltpu.roll(packed, g * top, 1)
    for n in range(lines):
        picked = jnp.where(line == group + n * per, jnp.where(group < per, spread, 0.0), 0.0)
        ssend[n] = jnp.sum(picked, axis=0)

    me = r * nc + c

    def sp(p):
        return remote(
            ssend, srecv.at[me], s_send.at[p], s_recv.at[me], p // nc, lax.rem(p, nc)
        )

    def each_device(fn):
        @pl.loop(1, nr * nc)
        def _(d):
            fn(lax.rem(me + d, nr * nc))

    each_device(lambda p: sp(p).start())
    srecv[me] = ssend[...]

    for t in range(terms):
        totals = [jnp.zeros((ev, width), jnp.float32) for _ in range(nc)]
        for k in range(slots):
            seen = colv[jnp.minimum(cols[0, t, 0, k], r)]
            moved = lax.dot_general(seen, w[t, k], LAST, preferred_element_type=jnp.float32)
            for a in range(nc):
                weight = jnp.where(rows[0, t, 0, k] == a, live[t * slots + k], 0.0)
                totals[a] += weight * moved
        for a in range(nc):
            fpart[a, t] = totals[a]

    def fp(p):
        return remote(fpart.at[p], frecv.at[c], f_send.at[p], f_recv.at[c], r, p)

    each_col(lambda p: fp(p).start())
    frecv[c] = fpart[c]

    def mp(j):
        return remote(
            msum.at[j], mrecv.at[q], m_send.at[j], m_recv.at[q], 2 * j + half, c
        )

    pp(0).wait_recv()
    msum[0] = mpart[half, 0] + pair[0]

    @pl.loop(1, q + 1)
    def _(j):
        pp(j).wait_recv()
        msum[j] = mpart[half, j] + pair[j]
        mp(j - 1).start()

    each_col(
        lambda p: remote(fpart.at[p], frecv.at[p], f_send.at[p], f_recv.at[p], r, p).wait_recv()
    )
    sums = frecv[0]
    for a in range(1, nc):
        sums += frecv[a]
    app_ref[...] = sums + msum[q]

    @pl.loop(q + 1, nr // 2)
    def _(s):
        remote(
            msum.at[s], mrecv.at[s], m_send.at[s], m_recv.at[s], 2 * s + half, c
        ).wait_recv()
        app_ref[...] += mrecv[s]

    each_device(
        lambda p: remote(
            ssend, srecv.at[p], s_send.at[p], s_recv.at[p], p // nc, lax.rem(p, nc)
        ).wait_recv()
    )
    whole = srecv[0]
    for s in range(1, nr * nc):
        whole += srecv[s]
    picked = jnp.zeros((ev, width), jnp.float32)
    for n in range(lines):
        picked += jnp.where(
            line == group + n * per,
            jnp.where(group < per, jnp.broadcast_to(whole[n : n + 1], (ev, width)), 0.0),
            0.0,
        )
    spread = picked
    for g in range(1, per):
        spread += pltpu.roll(picked, width - g * top, 1)
    for t in range(terms):
        sub_ref[t] = spread[:, t * ev : (t + 1) * ev] * scale

    each_col(lambda p: rv(p).wait_send())
    each_col(lambda p: fp(p).wait_send())
    each_device(lambda p: sp(p).wait_send())

    @pl.loop(0, nr - 1 - r)
    def _(i):
        cv(nr - 1 - i).wait_send()

    @pl.loop(0, q + 1)
    def _(j):
        pp(j).wait_send()

    @pl.loop(0, q)
    def _(j):
        mp(j).wait_send()


def flip(table):
    return jnp.swapaxes(table, 1, 2)


def shards(nr, nc, vectors, tile_vals, tile_rows, tile_cols, tile_counts, tile_diag):
    ev, width = vectors.shape
    terms, slots = tile_vals.shape[2], tile_vals.shape[3]
    f32 = jnp.float32
    scale = 1.0 / math.sqrt(width * nr * nc)
    vmem = pl.BlockSpec(memory_space=pltpu.VMEM)
    hbm = pl.BlockSpec(memory_space=pltpu.MemorySpace.HBM)
    top = terms * ev
    lines = -(-ev // (width // top))
    table = pltpu.SMEM((1, terms, 1, slots), jnp.int32)
    dma = pltpu.SemaphoreType.DMA
    return finish(*pl.pallas_call(
        functools.partial(kernel, nr, nc, scale),
        out_shape=(
            jax.ShapeDtypeStruct((terms, ev, width), f32),
            jax.ShapeDtypeStruct((terms, ev, ev), f32),
        ),
        in_specs=[hbm] * 6,
        out_specs=(vmem, vmem),
        scratch_shapes=[
            pltpu.VMEM(vectors.shape, vectors.dtype),
            table, table, pltpu.SMEM(tile_counts.shape, jnp.int32), table,
            pltpu.VMEM(tile_vals.shape[2:], tile_vals.dtype),
            pltpu.VMEM((nc, ev, width), vectors.dtype),
            pltpu.VMEM((nr, ev, width), vectors.dtype),
            pltpu.VMEM((terms, slots, ev, width), f32),
            pltpu.VMEM((terms, 3 * ev, slots * width), jnp.bfloat16),
            pltpu.VMEM((terms, 3 * ev, slots * width), jnp.bfloat16),
            pltpu.VMEM((2, nr // 2, terms, ev, width), f32),
            pltpu.VMEM((nr // 2, terms, ev, width), f32),
            pltpu.VMEM((nr // 2, terms, ev, width), f32),
            pltpu.VMEM((nr // 2, terms, ev, width), f32),
            pltpu.VMEM((nc, terms, ev, width), f32),
            pltpu.VMEM((nc, terms, ev, width), f32),
            pltpu.VMEM((lines, width), f32),
            pltpu.VMEM((nr * nc, lines, width), f32),
            dma((5,)), dma,
            dma((nc,)), dma((nc,)), dma((nr,)), dma((nr,)),
            dma((nr // 2,)), dma((nr // 2,)), dma((nr // 2,)), dma((nr // 2,)),
            dma((nc,)), dma((nc,)), dma((nr * nc,)), dma((nr * nc,)),
        ],
        compiler_params=pltpu.CompilerParams(collective_id=0, has_side_effects=True, vmem_limit_bytes=LIMIT),
    )(vectors, tile_vals, flip(tile_rows), flip(tile_cols), tile_counts, flip(tile_diag)))


def finish(applied, subspace):
    def body(a_ref, b_ref, c_ref, d_ref, sem):
        one = pltpu.make_async_copy(a_ref, c_ref, sem.at[0])
        two = pltpu.make_async_copy(b_ref, d_ref, sem.at[1])
        one.start()
        two.start()
        one.wait()
        two.wait()

    return pl.pallas_call(
        body,
        out_shape=(
            jax.ShapeDtypeStruct(applied.shape, applied.dtype),
            jax.ShapeDtypeStruct(subspace.shape, subspace.dtype),
        ),
        in_specs=[pl.BlockSpec(memory_space=pltpu.VMEM)] * 2,
        out_specs=(pl.BlockSpec(memory_space=pltpu.MemorySpace.HBM),) * 2,
        scratch_shapes=[pltpu.SemaphoreType.DMA((2,))],
        compiler_params=pltpu.CompilerParams(vmem_limit_bytes=LIMIT),
    )(applied, subspace)


def solution(mesh):
    placed = (
        P(None, ("row", "col")),
        P("row", "col", None, None, None, None),
        P("row", "col", None, None),
        P("row", "col", None, None),
        P("row", "col", None),
        P("row", "col", None, None),
    )
    return jax.shard_map(
        functools.partial(shards, mesh.shape["row"], mesh.shape["col"]),
        mesh=mesh,
        in_specs=placed,
        out_specs=(P(None, None, ("row", "col")), P()),
        check_vma=False,
    )
```

```python
import functools
import math

import jax
import jax.numpy as jnp
from jax import lax
from jax.experimental import pallas as pl
from jax.experimental.pallas import tpu as pltpu
from jax.sharding import PartitionSpec as P

MESH = pl.DeviceIdType.MESH
LAST = (((1,), (1,)), ((), ()))


def kernel(
    nr, nc, scale,
    v_hbm, w_hbm, rows_hbm, cols_hbm, counts_hbm, diag_hbm,
    app_ref, sub_ref,
    v_ref, rows, cols, counts, diag,
    w, rowv, colv, mterm, ahead, back, mpart, pair, msum, mrecv, fpart, frecv, ssend, srecv,
    in_sem, w_sem, rv_send, rv_recv, cv_send, cv_recv, p_send, p_recv, m_send, m_recv,
    f_send, f_recv, s_send, s_recv,
):
    r = lax.axis_index("row")
    c = lax.axis_index("col")
    q = r // 2
    half = lax.rem(r, 2)
    ev, width = v_ref.shape
    terms, slots = w.shape[0], w.shape[1]
    top = terms * ev

    def remote(src, dst, send, recv, row, col):
        return pltpu.make_async_remote_copy(
            src_ref=src, dst_ref=dst, send_sem=send, recv_sem=recv,
            device_id=(row, col), device_id_type=MESH,
        )

    def each_row(fn):
        @pl.loop(1, nr)
        def _(d):
            fn(lax.rem(r + d, nr))

    def each_col(fn):
        @pl.loop(1, nc)
        def _(d):
            fn(lax.rem(c + d, nc))

    barrier = pltpu.get_barrier_semaphore()
    each_row(lambda p: pl.semaphore_signal(barrier, inc=1, device_id=(p, c), device_id_type=MESH))
    each_col(lambda p: pl.semaphore_signal(barrier, inc=1, device_id=(r, p), device_id_type=MESH))

    small_in = [
        pltpu.make_async_copy(src, dst, in_sem.at[i])
        for i, (src, dst) in enumerate(
            [(v_hbm, v_ref), (rows_hbm, rows), (cols_hbm, cols), (counts_hbm, counts), (diag_hbm, diag)]
        )
    ]
    for copy in small_in:
        copy.start()
    w_copy = pltpu.make_async_copy(w_hbm.at[0, 0], w, w_sem)
    w_copy.start()
    zero = jnp.zeros((ev, width), v_ref.dtype)

    @pl.loop(r + 1, nr)
    def _(b):
        colv[b] = zero

    for copy in small_in:
        copy.wait()
    own = v_ref[...]
    rowv[c] = own
    colv[r] = own
    live = []
    off = []
    for t in range(terms):
        for k in range(slots):
            alive = k < counts[0, 0, t]
            live.append(jnp.where(alive, 1.0, 0.0).astype(jnp.float32))
            off.append(jnp.where(alive & (diag[0, t, 0, k] == 0), 1.0, 0.0).astype(jnp.float32))
    pl.semaphore_wait(barrier, nr - 1 + nc - 1)

    def rv(p):
        return remote(v_ref, rowv.at[c], rv_send.at[p], rv_recv.at[c], r, p)

    def cv(p):
        return remote(v_ref, colv.at[r], cv_send.at[p], cv_recv.at[r], p, c)

    each_col(lambda p: rv(p).start())

    @pl.loop(0, nr - 1 - r)
    def _(i):
        cv(nr - 1 - i).start()

    w_copy.wait()
    each_col(lambda p: remote(v_ref, rowv.at[p], rv_send.at[p], rv_recv.at[p], r, p).wait_recv())

    for t in range(terms):
        for k in range(slots):
            mterm[t, k] = jnp.dot(
                rowv[rows[0, t, 0, k]], w[t, k], preferred_element_type=jnp.float32
            )

    def place(side, j):
        b = 2 * j + side
        for t in range(terms):
            total = jnp.zeros((ev, width), jnp.float32)
            for k in range(slots):
                weight = jnp.where(cols[0, t, 0, k] == b, off[t * slots + k], 0.0)
                total += weight * mterm[t, k]
            mpart[side, j, t] = total

    def pp(j):
        return remote(
            mpart.at[1 - half, j], pair.at[j], p_send.at[j], p_recv.at[j], r + 1 - 2 * half, c
        )

    place(1 - half, 0)

    @pl.loop(1, q + 1)
    def _(j):
        place(1 - half, j)
        pp(j - 1).start()

    pp(q).start()

    @pl.loop(0, q + 1)
    def _(j):
        place(half, j)

    def parts(value):
        high = value.astype(jnp.bfloat16)
        rest = value - high.astype(jnp.float32)
        middle = rest.astype(jnp.bfloat16)
        low = (rest - middle.astype(jnp.float32)).astype(jnp.bfloat16)
        return jnp.concatenate([high, middle, low], axis=0)

    for t in range(terms):
        for k in range(slots):
            lanes = pl.ds(k * width, width)
            split = parts(mterm[t, k])
            ahead[t, :, lanes] = split * live[t * slots + k].astype(jnp.bfloat16)
            back[t, :, lanes] = split * off[t * slots + k].astype(jnp.bfloat16)

    @pl.loop(0, r)
    def _(b):
        remote(v_ref, colv.at[b], cv_send.at[b], cv_recv.at[b], b, c).wait_recv()

    small = []
    for t in range(terms):
        wide = jnp.concatenate(
            [colv[jnp.minimum(cols[0, t, 0, k], r)] for k in range(slots)], axis=1
        )
        one = lax.dot_general(ahead[t], wide, LAST, preferred_element_type=jnp.float32)
        two = lax.dot_general(wide, back[t], LAST, preferred_element_type=jnp.float32)
        small.append(
            (one[2 * ev :] + one[ev : 2 * ev]) + one[:ev]
            + ((two[:, 2 * ev :] + two[:, ev : 2 * ev]) + two[:, :ev])
        )
    small.append(jnp.zeros((ev, width - top), jnp.float32))
    packed = jnp.concatenate(small, axis=1)

    per = width // top
    lines = -(-ev // per)
    line = lax.broadcasted_iota(jnp.int32, (ev, width), 0)
    group = lax.broadcasted_iota(jnp.int32, (ev, width), 1) // top
    spread = packed
    for g in range(1, per):
        spread += pltpu.roll(packed, g * top, 1)
    for n in range(lines):
        picked = jnp.where(line == group + n * per, jnp.where(group < per, spread, 0.0), 0.0)
        ssend[n] = jnp.sum(picked, axis=0)

    me = r * nc + c

    def sp(p):
        return remote(
            ssend, srecv.at[me], s_send.at[p], s_recv.at[me], p // nc, lax.rem(p, nc)
        )

    def each_device(fn):
        @pl.loop(1, nr * nc)
        def _(d):
            fn(lax.rem(me + d, nr * nc))

    each_device(lambda p: sp(p).start())
    srecv[me] = ssend[...]

    for t in range(terms):
        totals = [jnp.zeros((ev, width), jnp.float32) for _ in range(nc)]
        for k in range(slots):
            seen = colv[jnp.minimum(cols[0, t, 0, k], r)]
            moved = lax.dot_general(seen, w[t, k], LAST, preferred_element_type=jnp.float32)
            for a in range(nc):
                weight = jnp.where(rows[0, t, 0, k] == a, live[t * slots + k], 0.0)
                totals[a] += weight * moved
        for a in range(nc):
            fpart[a, t] = totals[a]

    def fp(p):
        return remote(fpart.at[p], frecv.at[c], f_send.at[p], f_recv.at[c], r, p)

    each_col(lambda p: fp(p).start())
    frecv[c] = fpart[c]

    def mp(j):
        return remote(
            msum.at[j], mrecv.at[q], m_send.at[j], m_recv.at[q], 2 * j + half, c
        )

    pp(0).wait_recv()
    msum[0] = mpart[half, 0] + pair[0]

    @pl.loop(1, q + 1)
    def _(j):
        pp(j).wait_recv()
        msum[j] = mpart[half, j] + pair[j]
        mp(j - 1).start()

    each_col(
        lambda p: remote(fpart.at[p], frecv.at[p], f_send.at[p], f_recv.at[p], r, p).wait_recv()
    )
    sums = frecv[0]
    for a in range(1, nc):
        sums += frecv[a]
    app_ref[...] = sums + msum[q]

    @pl.loop(q + 1, nr // 2)
    def _(s):
        remote(
            msum.at[s], mrecv.at[s], m_send.at[s], m_recv.at[s], 2 * s + half, c
        ).wait_recv()
        app_ref[...] += mrecv[s]

    each_device(
        lambda p: remote(
            ssend, srecv.at[p], s_send.at[p], s_recv.at[p], p // nc, lax.rem(p, nc)
        ).wait_recv()
    )
    whole = srecv[0]
    for s in range(1, nr * nc):
        whole += srecv[s]
    picked = jnp.zeros((ev, width), jnp.float32)
    for n in range(lines):
        picked += jnp.where(
            line == group + n * per,
            jnp.where(group < per, jnp.broadcast_to(whole[n : n + 1], (ev, width)), 0.0),
            0.0,
        )
    spread = picked
    for g in range(1, per):
        spread += pltpu.roll(picked, width - g * top, 1)
    for t in range(terms):
        sub_ref[t] = spread[:, t * ev : (t + 1) * ev] * scale

    each_col(lambda p: rv(p).wait_send())
    each_col(lambda p: fp(p).wait_send())
    each_device(lambda p: sp(p).wait_send())

    @pl.loop(0, nr - 1 - r)
    def _(i):
        cv(nr - 1 - i).wait_send()

    @pl.loop(0, q + 1)
    def _(j):
        pp(j).wait_send()

    @pl.loop(0, q)
    def _(j):
        mp(j).wait_send()


def flip(table):
    return jnp.swapaxes(table, 1, 2)


def shards(nr, nc, vectors, tile_vals, tile_rows, tile_cols, tile_counts, tile_diag):
    ev, width = vectors.shape
    terms, slots = tile_vals.shape[2], tile_vals.shape[3]
    f32 = jnp.float32
    scale = 1.0 / math.sqrt(width * nr * nc)
    vmem = pl.BlockSpec(memory_space=pltpu.VMEM)
    hbm = pl.BlockSpec(memory_space=pltpu.MemorySpace.HBM)
    top = terms * ev
    lines = -(-ev // (width // top))
    table = pltpu.SMEM((1, terms, 1, slots), jnp.int32)
    dma = pltpu.SemaphoreType.DMA
    return finish(*pl.pallas_call(
        functools.partial(kernel, nr, nc, scale),
        out_shape=(
            pltpu.VMEM((terms, ev, width), f32),
            pltpu.VMEM((terms, ev, ev), f32),
        ),
        in_specs=[hbm] * 6,
        out_specs=(vmem, vmem),
        scratch_shapes=[
            pltpu.VMEM(vectors.shape, vectors.dtype),
            table, table, pltpu.SMEM(tile_counts.shape, jnp.int32), table,
            pltpu.VMEM(tile_vals.shape[2:], tile_vals.dtype),
            pltpu.VMEM((nc, ev, width), vectors.dtype),
            pltpu.VMEM((nr, ev, width), vectors.dtype),
            pltpu.VMEM((terms, slots, ev, width), f32),
            pltpu.VMEM((terms, 3 * ev, slots * width), jnp.bfloat16),
            pltpu.VMEM((terms, 3 * ev, slots * width), jnp.bfloat16),
            pltpu.VMEM((2, nr // 2, terms, ev, width), f32),
            pltpu.VMEM((nr // 2, terms, ev, width), f32),
            pltpu.VMEM((nr // 2, terms, ev, width), f32),
            pltpu.VMEM((nr // 2, terms, ev, width), f32),
            pltpu.VMEM((nc, terms, ev, width), f32),
            pltpu.VMEM((nc, terms, ev, width), f32),
            pltpu.VMEM((lines, width), f32),
            pltpu.VMEM((nr * nc, lines, width), f32),
            dma((5,)), dma,
            dma((nc,)), dma((nc,)), dma((nr,)), dma((nr,)),
            dma((nr // 2,)), dma((nr // 2,)), dma((nr // 2,)), dma((nr // 2,)),
            dma((nc,)), dma((nc,)), dma((nr * nc,)), dma((nr * nc,)),
        ],
        compiler_params=pltpu.CompilerParams(collective_id=0, has_side_effects=True),
    )(vectors, tile_vals, flip(tile_rows), flip(tile_cols), tile_counts, flip(tile_diag)))


def finish(applied, subspace):
    def body(a_ref, b_ref, c_ref, d_ref, sem):
        one = pltpu.make_async_copy(a_ref, c_ref, sem.at[0])
        two = pltpu.make_async_copy(b_ref, d_ref, sem.at[1])
        one.start()
        two.start()
        one.wait()
        two.wait()

    return pl.pallas_call(
        body,
        out_shape=(
            jax.ShapeDtypeStruct(applied.shape, applied.dtype),
            jax.ShapeDtypeStruct(subspace.shape, subspace.dtype),
        ),
        in_specs=[pl.BlockSpec(memory_space=pltpu.VMEM)] * 2,
        out_specs=(pl.BlockSpec(memory_space=pltpu.MemorySpace.HBM),) * 2,
        scratch_shapes=[pltpu.SemaphoreType.DMA((2,))],
        compiler_params=pltpu.CompilerParams(vmem_limit_bytes=2**20),
    )(applied, subspace)


def solution(mesh):
    placed = (
        P(None, ("row", "col")),
        P("row", "col", None, None, None, None),
        P("row", "col", None, None),
        P("row", "col", None, None),
        P("row", "col", None),
        P("row", "col", None, None),
    )
    return jax.shard_map(
        functools.partial(shards, mesh.shape["row"], mesh.shape["col"]),
        mesh=mesh,
        in_specs=placed,
        out_specs=(P(None, None, ("row", "col")), P()),
        check_vma=False,
    )
```

```python
import functools
import math

import jax
import jax.numpy as jnp
from jax import lax
from jax.experimental import pallas as pl
from jax.experimental.pallas import tpu as pltpu
from jax.sharding import PartitionSpec as P

MESH = pl.DeviceIdType.MESH
LAST = (((1,), (1,)), ((), ()))


def kernel(
    nr, nc, scale,
    v_hbm, w_hbm, rows_hbm, cols_hbm, counts_hbm, diag_hbm,
    app_ref, sub_ref,
    v_ref, rows, cols, counts, diag,
    w, rowv, colv, mterm, ahead, back, mpart, pair, msum, mrecv, fpart, frecv, ssend, srecv,
    in_sem, w_sem, rv_send, rv_recv, cv_send, cv_recv, p_send, p_recv, m_send, m_recv,
    f_send, f_recv, s_send, s_recv,
):
    r = lax.axis_index("row")
    c = lax.axis_index("col")
    q = r // 2
    half = lax.rem(r, 2)
    ev, width = v_ref.shape
    terms, slots = w.shape[0], w.shape[1]
    top = terms * ev

    def remote(src, dst, send, recv, row, col):
        return pltpu.make_async_remote_copy(
            src_ref=src, dst_ref=dst, send_sem=send, recv_sem=recv,
            device_id=(row, col), device_id_type=MESH,
        )

    def each_row(fn):
        @pl.loop(1, nr)
        def _(d):
            fn(lax.rem(r + d, nr))

    def each_col(fn):
        @pl.loop(1, nc)
        def _(d):
            fn(lax.rem(c + d, nc))

    barrier = pltpu.get_barrier_semaphore()
    each_row(lambda p: pl.semaphore_signal(barrier, inc=1, device_id=(p, c), device_id_type=MESH))
    each_col(lambda p: pl.semaphore_signal(barrier, inc=1, device_id=(r, p), device_id_type=MESH))

    small_in = [
        pltpu.make_async_copy(src, dst, in_sem.at[i])
        for i, (src, dst) in enumerate(
            [(v_hbm, v_ref), (rows_hbm, rows), (cols_hbm, cols), (counts_hbm, counts), (diag_hbm, diag)]
        )
    ]
    for copy in small_in:
        copy.start()
    w_copy = pltpu.make_async_copy(w_hbm.at[0, 0], w, w_sem)
    w_copy.start()
    zero = jnp.zeros((ev, width), v_ref.dtype)

    @pl.loop(r + 1, nr)
    def _(b):
        colv[b] = zero

    for copy in small_in:
        copy.wait()
    own = v_ref[...]
    rowv[c] = own
    colv[r] = own
    live = []
    off = []
    for t in range(terms):
        for k in range(slots):
            alive = k < counts[0, 0, t]
            live.append(jnp.where(alive, 1.0, 0.0).astype(jnp.float32))
            off.append(jnp.where(alive & (diag[0, t, 0, k] == 0), 1.0, 0.0).astype(jnp.float32))
    pl.semaphore_wait(barrier, nr - 1 + nc - 1)

    def rv(p):
        return remote(v_ref, rowv.at[c], rv_send.at[p], rv_recv.at[c], r, p)

    def cv(p):
        return remote(v_ref, colv.at[r], cv_send.at[p], cv_recv.at[r], p, c)

    each_col(lambda p: rv(p).start())

    @pl.loop(0, nr - 1 - r)
    def _(i):
        cv(nr - 1 - i).start()

    w_copy.wait()
    each_col(lambda p: remote(v_ref, rowv.at[p], rv_send.at[p], rv_recv.at[p], r, p).wait_recv())

    for t in range(terms):
        for k in range(slots):
            mterm[t, k] = jnp.dot(
                rowv[rows[0, t, 0, k]], w[t, k], preferred_element_type=jnp.float32
            )

    def place(side, j):
        b = 2 * j + side
        for t in range(terms):
            total = jnp.zeros((ev, width), jnp.float32)
            for k in range(slots):
                weight = jnp.where(cols[0, t, 0, k] == b, off[t * slots + k], 0.0)
                total += weight * mterm[t, k]
            mpart[side, j, t] = total

    def pp(j):
        return remote(
            mpart.at[1 - half, j], pair.at[j], p_send.at[j], p_recv.at[j], r + 1 - 2 * half, c
        )

    place(1 - half, 0)

    @pl.loop(1, q + 1)
    def _(j):
        place(1 - half, j)
        pp(j - 1).start()

    pp(q).start()

    @pl.loop(0, q + 1)
    def _(j):
        place(half, j)

    def parts(value):
        high = value.astype(jnp.bfloat16)
        rest = value - high.astype(jnp.float32)
        middle = rest.astype(jnp.bfloat16)
        low = (rest - middle.astype(jnp.float32)).astype(jnp.bfloat16)
        return jnp.concatenate([high, middle, low], axis=0)

    for t in range(terms):
        for k in range(slots):
            lanes = pl.ds(k * width, width)
            split = parts(mterm[t, k])
            ahead[t, :, lanes] = split * live[t * slots + k].astype(jnp.bfloat16)
            back[t, :, lanes] = split * off[t * slots + k].astype(jnp.bfloat16)

    @pl.loop(0, r)
    def _(b):
        remote(v_ref, colv.at[b], cv_send.at[b], cv_recv.at[b], b, c).wait_recv()

    small = []
    for t in range(terms):
        wide = jnp.concatenate(
            [colv[jnp.minimum(cols[0, t, 0, k], r)] for k in range(slots)], axis=1
        )
        one = lax.dot_general(ahead[t], wide, LAST, preferred_element_type=jnp.float32)
        two = lax.dot_general(wide, back[t], LAST, preferred_element_type=jnp.float32)
        small.append(
            (one[2 * ev :] + one[ev : 2 * ev]) + one[:ev]
            + ((two[:, 2 * ev :] + two[:, ev : 2 * ev]) + two[:, :ev])
        )
    small.append(jnp.zeros((ev, width - top), jnp.float32))
    packed = jnp.concatenate(small, axis=1)

    per = width // top
    lines = -(-ev // per)
    line = lax.broadcasted_iota(jnp.int32, (ev, width), 0)
    group = lax.broadcasted_iota(jnp.int32, (ev, width), 1) // top
    spread = packed
    for g in range(1, per):
        spread += pltpu.roll(packed, g * top, 1)
    for n in range(lines):
        picked = jnp.where(line == group + n * per, jnp.where(group < per, spread, 0.0), 0.0)
        ssend[n] = jnp.sum(picked, axis=0)

    me = r * nc + c

    def sp(p):
        return remote(
            ssend, srecv.at[me], s_send.at[p], s_recv.at[me], p // nc, lax.rem(p, nc)
        )

    def each_device(fn):
        @pl.loop(1, nr * nc)
        def _(d):
            fn(lax.rem(me + d, nr * nc))

    each_device(lambda p: sp(p).start())
    srecv[me] = ssend[...]

    def mp(j):
        return remote(
            msum.at[j], mrecv.at[q], m_send.at[j], m_recv.at[q], 2 * j + half, c
        )

    pp(0).wait_recv()
    msum[0] = mpart[half, 0] + pair[0]

    @pl.loop(1, q + 1)
    def _(j):
        pp(j).wait_recv()
        msum[j] = mpart[half, j] + pair[j]
        mp(j - 1).start()

    for t in range(terms):
        totals = [jnp.zeros((ev, width), jnp.float32) for _ in range(nc)]
        for k in range(slots):
            seen = colv[jnp.minimum(cols[0, t, 0, k], r)]
            moved = lax.dot_general(seen, w[t, k], LAST, preferred_element_type=jnp.float32)
            for a in range(nc):
                weight = jnp.where(rows[0, t, 0, k] == a, live[t * slots + k], 0.0)
                totals[a] += weight * moved
        for a in range(nc):
            fpart[a, t] = totals[a]

    def fp(p):
        return remote(fpart.at[p], frecv.at[c], f_send.at[p], f_recv.at[c], r, p)

    each_col(lambda p: fp(p).start())
    frecv[c] = fpart[c]

    each_col(
        lambda p: remote(fpart.at[p], frecv.at[p], f_send.at[p], f_recv.at[p], r, p).wait_recv()
    )
    sums = frecv[0]
    for a in range(1, nc):
        sums += frecv[a]
    app_ref[...] = sums + msum[q]

    @pl.loop(q + 1, nr // 2)
    def _(s):
        remote(
            msum.at[s], mrecv.at[s], m_send.at[s], m_recv.at[s], 2 * s + half, c
        ).wait_recv()
        app_ref[...] += mrecv[s]

    each_device(
        lambda p: remote(
            ssend, srecv.at[p], s_send.at[p], s_recv.at[p], p // nc, lax.rem(p, nc)
        ).wait_recv()
    )
    whole = srecv[0]
    for s in range(1, nr * nc):
        whole += srecv[s]
    picked = jnp.zeros((ev, width), jnp.float32)
    for n in range(lines):
        picked += jnp.where(
            line == group + n * per,
            jnp.where(group < per, jnp.broadcast_to(whole[n : n + 1], (ev, width)), 0.0),
            0.0,
        )
    spread = picked
    for g in range(1, per):
        spread += pltpu.roll(picked, width - g * top, 1)
    for t in range(terms):
        sub_ref[t] = spread[:, t * ev : (t + 1) * ev] * scale

    each_col(lambda p: rv(p).wait_send())
    each_col(lambda p: fp(p).wait_send())
    each_device(lambda p: sp(p).wait_send())

    @pl.loop(0, nr - 1 - r)
    def _(i):
        cv(nr - 1 - i).wait_send()

    @pl.loop(0, q + 1)
    def _(j):
        pp(j).wait_send()

    @pl.loop(0, q)
    def _(j):
        mp(j).wait_send()


def flip(table):
    return jnp.swapaxes(table, 1, 2)


def shards(nr, nc, vectors, tile_vals, tile_rows, tile_cols, tile_counts, tile_diag):
    ev, width = vectors.shape
    terms, slots = tile_vals.shape[2], tile_vals.shape[3]
    f32 = jnp.float32
    scale = 1.0 / math.sqrt(width * nr * nc)
    vmem = pl.BlockSpec(memory_space=pltpu.VMEM)
    hbm = pl.BlockSpec(memory_space=pltpu.MemorySpace.HBM)
    top = terms * ev
    lines = -(-ev // (width // top))
    table = pltpu.SMEM((1, terms, 1, slots), jnp.int32)
    dma = pltpu.SemaphoreType.DMA
    return finish(*pl.pallas_call(
        functools.partial(kernel, nr, nc, scale),
        out_shape=(
            pltpu.VMEM((terms, ev, width), f32),
            pltpu.VMEM((terms, ev, ev), f32),
        ),
        in_specs=[hbm] * 6,
        out_specs=(vmem, vmem),
        scratch_shapes=[
            pltpu.VMEM(vectors.shape, vectors.dtype),
            table, table, pltpu.SMEM(tile_counts.shape, jnp.int32), table,
            pltpu.VMEM(tile_vals.shape[2:], tile_vals.dtype),
            pltpu.VMEM((nc, ev, width), vectors.dtype),
            pltpu.VMEM((nr, ev, width), vectors.dtype),
            pltpu.VMEM((terms, slots, ev, width), f32),
            pltpu.VMEM((terms, 3 * ev, slots * width), jnp.bfloat16),
            pltpu.VMEM((terms, 3 * ev, slots * width), jnp.bfloat16),
            pltpu.VMEM((2, nr // 2, terms, ev, width), f32),
            pltpu.VMEM((nr // 2, terms, ev, width), f32),
            pltpu.VMEM((nr // 2, terms, ev, width), f32),
            pltpu.VMEM((nr // 2, terms, ev, width), f32),
            pltpu.VMEM((nc, terms, ev, width), f32),
            pltpu.VMEM((nc, terms, ev, width), f32),
            pltpu.VMEM((lines, width), f32),
            pltpu.VMEM((nr * nc, lines, width), f32),
            dma((5,)), dma,
            dma((nc,)), dma((nc,)), dma((nr,)), dma((nr,)),
            dma((nr // 2,)), dma((nr // 2,)), dma((nr // 2,)), dma((nr // 2,)),
            dma((nc,)), dma((nc,)), dma((nr * nc,)), dma((nr * nc,)),
        ],
        compiler_params=pltpu.CompilerParams(collective_id=0, has_side_effects=True),
    )(vectors, tile_vals, flip(tile_rows), flip(tile_cols), tile_counts, flip(tile_diag)))


def finish(applied, subspace):
    def body(a_ref, b_ref, c_ref, d_ref, sem):
        one = pltpu.make_async_copy(a_ref, c_ref, sem.at[0])
        two = pltpu.make_async_copy(b_ref, d_ref, sem.at[1])
        one.start()
        two.start()
        one.wait()
        two.wait()

    return pl.pallas_call(
        body,
        out_shape=(
            jax.ShapeDtypeStruct(applied.shape, applied.dtype),
            jax.ShapeDtypeStruct(subspace.shape, subspace.dtype),
        ),
        in_specs=[pl.BlockSpec(memory_space=pltpu.VMEM)] * 2,
        out_specs=(pl.BlockSpec(memory_space=pltpu.MemorySpace.HBM),) * 2,
        scratch_shapes=[pltpu.SemaphoreType.DMA((2,))],
        compiler_params=pltpu.CompilerParams(vmem_limit_bytes=2**20),
    )(applied, subspace)


def solution(mesh):
    placed = (
        P(None, ("row", "col")),
        P("row", "col", None, None, None, None),
        P("row", "col", None, None),
        P("row", "col", None, None),
        P("row", "col", None),
        P("row", "col", None, None),
    )
    return jax.shard_map(
        functools.partial(shards, mesh.shape["row"], mesh.shape["col"]),
        mesh=mesh,
        in_specs=placed,
        out_specs=(P(None, None, ("row", "col")), P()),
        check_vma=False,
    )
```
